32 devices in a mesh: angle: 4 (over z), strip: 8 (over y, x, core).
Axes of the slice: x: 2, y: 2, z: 4, core: 2. Of those that a mesh axis runs over, the one named last changes fastest.
Arguments:
- object_field: float32 [2, 4, 1024, 1024], P(None, 'angle', 'strip'), may hold values from -5 to 5
- amplitudes: bfloat16 [4, 32, 256, 256], P('angle', 'strip'), may hold values from 0.25 to 4
- scan_offsets: int32 [4, 32, 2], P('angle', 'strip'), may hold values from 0 to 768, as said below
- probe_field: float32 [2, 256, 256], replicated, may hold values from -5 to 5
- tilt_angles: float32 [4], replicated, may hold values from -3.140625 to 3.140625
Outputs:
- object_grad: float32 [2, 4, 1024, 1024], P(None, 'angle', 'strip')
- probe_grad: float32 [2, 256, 256], replicated
- volume_grad: float32 [8, 4, 32, 16384], P('strip', 'angle')
The draws below stay inside these ranges and needn't reach their ends.
Inputs may be any that keep to these rules, and one draw needn't show every extreme that they name: `scan_offsets`: row offsets lie in 0 to 0 and column offsets in 0 to 768. In every strip's block of 4 frames, the first frame has row offset 0 and column offset 768, the second row offset 0 and column offset 0, the third column offset 768 // 2.
All inputs are finite; a program needn't handle non-finite values.
Results may differ from the reference program's by a relative error of at most 0.0079.
The reference program's roundings to bfloat16 on the way count: a program that leaves them out, or rounds other values in their place, can miss the bound.
Values may be sent and summed in bfloat16 or wider, within the bound.
No kernel may reach another device: no remote copies, remote signals or barrier semaphores. Data moves between devices by JAX's collectives and lax.ppermute only.
A program may use at most 64 MiB of HBM per device.

```python
import math
import jax
import jax.numpy as jnp
from jax import lax

W = 1024
FRAME = 256
HALO = 64
SR = 128
FRAMES = 4
NG = 128
CELLS = 16384
ANGLES = 4
STRIPS = 8
Z = 1024
FRAMES_ALL = 32
SLICES_DEV = 32
ROWSPAN = 0
COLSPAN = 768


def draw_scan_offsets(key, part):
    key_rows, key_cols = jax.random.split(jax.random.fold_in(key, 17))
    row_offsets = jax.random.randint(key_rows, (ANGLES, STRIPS, FRAMES), 0, ROWSPAN + 1, dtype=jnp.int32)
    col_offsets = jax.random.randint(key_cols, (ANGLES, STRIPS, FRAMES), 0, COLSPAN + 1, dtype=jnp.int32)
    row_offsets = row_offsets.at[:, :, 0].set(0).at[:, :, 1].set(ROWSPAN)
    col_offsets = col_offsets.at[:, :, 0].set(COLSPAN).at[:, :, 1].set(0).at[:, :, 2].set(COLSPAN // 2)
    stacked = jnp.stack([row_offsets, col_offsets], -1)
    return stacked.reshape(ANGLES, STRIPS * FRAMES, 2).astype(jnp.int32)


def level_of(own_key, extent, cuts, low, largest):
    gain, own = 1.0, jax.random.fold_in(own_key, 6)
    for axis_at, blocks in cuts:
        heights = jnp.exp(jax.random.uniform(jax.random.fold_in(own, axis_at), (blocks,), jnp.float32, low / len(cuts), largest / len(cuts)))
        gain = gain * jnp.repeat(heights, extent[axis_at] // blocks).reshape([-1 if axis == axis_at else 1 for axis in range(len(extent))])
    return gain


def gaussian(stream_key, extent, width, reach, pieces=(), kind=jnp.bfloat16):
    gain = level_of(stream_key, extent, pieces, -0.22, 0.18) if pieces else 1.0
    array = jax.random.normal(stream_key, extent, jnp.float32) * width * gain
    return jnp.minimum(jnp.maximum(array, -reach), reach).astype(kind)


def setup_inputs(seed: int = 0) -> dict:
    key_list = jax.random.split(jax.random.key(seed), 6)
    return {
        "object_field": gaussian(key_list[0], (2, ANGLES, Z, W), 0.7, 5.0, ((1, 4), (2, 8)), jnp.float32),
        "amplitudes": jnp.clip(jnp.exp(math.log(4.0) - 2.7725887 * jax.random.uniform(key_list[1], (ANGLES, FRAMES_ALL, FRAME, FRAME), jnp.float32) ** level_of(key_list[1], (ANGLES, FRAMES_ALL, FRAME, FRAME), ((0, 4), (1, 8)), -0.2, 0.2)), 0.25, 4.0).astype(jnp.bfloat16),
        "scan_offsets": draw_scan_offsets(jax.random.fold_in(key_list[5], 71), 0),
        "probe_field": gaussian(key_list[3], (2, FRAME, FRAME), 0.7, 5.0, (), jnp.float32),
        "tilt_angles": jnp.clip(jax.random.uniform(key_list[4], (ANGLES,), jnp.float32, -3.140625, 3.140625), -3.140625, 3.140625),
    }


def dft_tables(size_n):
    indices = jnp.arange(size_n, dtype=jnp.int32)
    product = indices[:, None] * indices[None, :] % size_n
    phase_arg = 2.0 * math.pi / size_n * product.astype(jnp.float32)
    norm_scale = 1.0 / math.sqrt(size_n)
    cos_tab = jnp.cos(phase_arg) * norm_scale
    sin_tab = jnp.sin(phase_arg) * norm_scale
    left_fwd = jnp.stack([jnp.stack([cos_tab, sin_tab]), jnp.stack([-sin_tab, cos_tab])]).astype(jnp.bfloat16)
    right_fwd = jnp.stack([jnp.stack([cos_tab, -sin_tab]), jnp.stack([sin_tab, cos_tab])]).astype(jnp.bfloat16)
    return (left_fwd, right_fwd)

def frame_grads(patches, probe_field, amp_block, left_fwd, right_fwd):
    probe_re, probe_im = (probe_field[0], probe_field[1])
    patch_re, patch_im = (patches[:, 0], patches[:, 1])
    exit_wave = jnp.stack([probe_re * patch_re - probe_im * patch_im, probe_re * patch_im + probe_im * patch_re], 1).astype(jnp.bfloat16)
    half = jnp.einsum('abik,fbkj->faij', left_fwd.astype(jnp.float32), exit_wave.astype(jnp.float32)).astype(jnp.bfloat16)
    wave = jnp.einsum('fbik,bakj->faij', half.astype(jnp.float32), right_fwd.astype(jnp.float32))
    magnitude_sq = wave[:, 0] * wave[:, 0] + wave[:, 1] * wave[:, 1]
    factor = 1.0 - amp_block.astype(jnp.float32) / jnp.sqrt(magnitude_sq + 1.0)
    misfit = (wave * factor[:, None]).astype(jnp.bfloat16)
    back = jnp.einsum('abik,fbkj->faij', right_fwd.astype(jnp.float32), misfit.astype(jnp.float32)).astype(jnp.bfloat16)
    exit_grad = jnp.einsum('fbik,bakj->faij', back.astype(jnp.float32), left_fwd.astype(jnp.float32))
    grad_re, grad_im = (exit_grad[:, 0], exit_grad[:, 1])
    object_terms = jnp.stack([probe_re * grad_re + probe_im * grad_im, probe_re * grad_im - probe_im * grad_re], 1)
    probe_terms = jnp.stack([lax.optimization_barrier(jnp.sum(patch_re * grad_re + patch_im * grad_im, 0)), lax.optimization_barrier(jnp.sum(patch_re * grad_im - patch_im * grad_re, 0))])
    return (object_terms, probe_terms)

def slice_project(rows, theta, side_cells, width_cols):
    cell = jnp.arange(side_cells * side_cells, dtype=jnp.int32)
    center = (side_cells - 1) / 2.0
    xpos = (cell // side_cells).astype(jnp.float32) - center
    ypos = (cell % side_cells).astype(jnp.float32) - center
    upos = (width_cols - 1) / 2.0 + 2.0 * (xpos * jnp.cos(theta) + ypos * jnp.sin(theta))
    lower = jnp.clip(jnp.floor(upos), 0.0, width_cols - 2.0)
    frac = upos - lower
    lower_idx = lower.astype(jnp.int32)
    left = jnp.take(rows, lower_idx, axis=1).astype(jnp.float32)
    right = jnp.take(rows, lower_idx + 1, axis=1).astype(jnp.float32)
    return left * (1.0 - frac) + right * frac

def reference(object_field, amplitudes, scan_offsets, probe_field, tilt_angles):
    left_fwd, right_fwd = dft_tables(FRAME)
    padded = jnp.pad(object_field, ((0, 0), (0, 0), (HALO, HALO), (0, 0)))
    ext_rows = SR + 2 * HALO

    def strip_work(flat_idx):
        angle_idx = (flat_idx // STRIPS).astype(jnp.int32)
        strip_idx = (flat_idx % STRIPS).astype(jnp.int32)
        zero_idx = jnp.int32(0)
        extended = lax.dynamic_slice(padded, (zero_idx, angle_idx, (strip_idx * SR).astype(jnp.int32), zero_idx), (2, 1, ext_rows, W))[:, 0]
        offsets = lax.dynamic_slice(scan_offsets, (angle_idx, (strip_idx * FRAMES).astype(jnp.int32), zero_idx), (1, FRAMES, 2))[0]
        amp_block = lax.dynamic_slice(amplitudes, (angle_idx, (strip_idx * FRAMES).astype(jnp.int32), zero_idx, zero_idx), (1, FRAMES, FRAME, FRAME))[0]

        def take_patch(offset_pair):
            return lax.dynamic_slice(extended, (zero_idx, offset_pair[0].astype(jnp.int32), offset_pair[1].astype(jnp.int32)), (2, FRAME, FRAME))
        patches = jax.vmap(take_patch)(offsets)
        object_terms, probe_terms = frame_grads(patches, probe_field, amp_block, left_fwd, right_fwd)

        def add_frame(frame_idx, accum):
            row_at = offsets[frame_idx, 0].astype(jnp.int32)
            col_at = offsets[frame_idx, 1].astype(jnp.int32)
            current = lax.dynamic_slice(accum, (zero_idx, row_at, col_at), (2, FRAME, FRAME))
            return lax.dynamic_update_slice(accum, current + object_terms[frame_idx], (zero_idx, row_at, col_at))
        ext_grad = lax.fori_loop(0, FRAMES, add_frame, jnp.zeros((2, ext_rows, W), jnp.float32))
        return (ext_grad, probe_terms)
    ext_all, probe_all = lax.map(strip_work, jnp.arange(ANGLES * STRIPS, dtype=jnp.int32))
    ext_all = ext_all.reshape(ANGLES, STRIPS, 2, ext_rows, W)
    core = ext_all[:, :, :, HALO:HALO + SR]
    from_above = jnp.pad(ext_all[:, 1:, :, :HALO], ((0, 0), (0, 1), (0, 0), (0, 0), (0, 0)))
    from_below = jnp.pad(ext_all[:, :-1, :, SR + HALO:], ((0, 0), (1, 0), (0, 0), (0, 0), (0, 0)))
    core = core.at[:, :, :, SR - HALO:].add(from_above)
    core = core.at[:, :, :, :HALO].add(from_below)
    object_grad = core.transpose(2, 0, 1, 3, 4).reshape(2, ANGLES, Z, W)
    probe_grad = lax.optimization_barrier(jnp.sum(probe_all, 0)) * (1.0 / math.sqrt(ANGLES * STRIPS * FRAMES))
    phase = (object_field[0] * object_grad[1] - object_field[1] * object_grad[0]).astype(jnp.bfloat16)

    def slab_work(block_idx):
        zero_idx = jnp.int32(0)

        def add_angle(angle_idx, total_sum):
            angle_at = jnp.asarray(angle_idx).astype(jnp.int32)
            rows = lax.dynamic_slice(phase, (angle_at, (block_idx * SLICES_DEV).astype(jnp.int32), zero_idx), (1, SLICES_DEV, W))[0]
            return total_sum + slice_project(rows, tilt_angles[angle_at], NG, W)
        return lax.fori_loop(0, ANGLES, add_angle, jnp.zeros((SLICES_DEV, CELLS), jnp.float32))
    volume = lax.map(slab_work, jnp.arange(Z // SLICES_DEV, dtype=jnp.int32))
    volume_grad = volume.reshape(STRIPS, ANGLES, SLICES_DEV, CELLS)
    return (object_grad, probe_grad, volume_grad)
```

```python
import functools
import math

import jax
import jax.numpy as jnp
import numpy as np
from jax import lax
from jax.experimental import pallas as pl
from jax.experimental.pallas import tpu as pltpu
from jax.sharding import PartitionSpec as P

HALO = 64
NG = 128
LANES = 128
GROUP = 8
F32 = jnp.float32
BF16 = jnp.bfloat16


def dft_blocks(size):
    k = np.arange(size)
    arg = 2.0 * np.pi / size * ((k[:, None] * k[None, :]) % size)
    c = np.cos(arg) / math.sqrt(size)
    s = np.sin(arg) / math.sqrt(size)
    fwd = np.block([[c, s], [-s, c]]).astype(np.float32).astype(jnp.bfloat16)
    inv = np.block([[c, -s], [s, c]]).astype(np.float32).astype(jnp.bfloat16)
    return fwd, inv


def frames_kernel(off_ref, own_ref, low_ref, high_ref, probe_ref, amp_ref, fwd_ref, inv_ref,
                  core_ref, rimw_ref, rimr_ref, pterm_ref, ext_ref, grad_ref, *, wlo, whi):
    nf, n, _ = amp_ref.shape
    rows = own_ref.shape[1]
    width = own_ref.shape[2]
    wide = n + LANES
    ext_ref[:, 0:HALO] = low_ref[...].astype(F32)
    ext_ref[:, HALO : HALO + rows] = own_ref[...]
    ext_ref[:, HALO + rows :] = high_ref[...].astype(F32)
    grad_ref[...] = jnp.zeros_like(grad_ref)
    pterm_ref[...] = jnp.zeros_like(pterm_ref)
    static_cols = (width - n, 0, (width - n) // 2)
    for f in range(nf):
        if f < 3 and static_cols[f] % LANES == 0:
            col, shift = static_cols[f], None
            patch_re = ext_ref[0, :, col : col + n]
            patch_im = ext_ref[1, :, col : col + n]
        else:
            at = off_ref[f, 1]
            base = pl.multiple_of(jnp.minimum((at >> 7) * LANES, width - wide), LANES)
            shift = at - base
            patch_re = pltpu.roll(ext_ref[0, :, pl.ds(base, wide)], wide - shift, axis=1)[:, :n]
            patch_im = pltpu.roll(ext_ref[1, :, pl.ds(base, wide)], wide - shift, axis=1)[:, :n]
        probe_re, probe_im = probe_ref[0], probe_ref[1]
        exit_wave = jnp.concatenate(
            [probe_re * patch_re - probe_im * patch_im, probe_re * patch_im + probe_im * patch_re], 0
        ).astype(BF16)
        half = jnp.dot(fwd_ref[...], exit_wave, preferred_element_type=F32).astype(BF16)
        half = jnp.concatenate([half[:n], half[n:]], 1)
        wave = jnp.dot(half, inv_ref[...], preferred_element_type=F32)
        wave_re, wave_im = wave[:, :n], wave[:, n:]
        factor = 1.0 - amp_ref[f].astype(F32) * lax.rsqrt(wave_re * wave_re + wave_im * wave_im + 1.0)
        misfit = jnp.concatenate([wave_re * factor, wave_im * factor], 0).astype(BF16)
        back = jnp.dot(inv_ref[...], misfit, preferred_element_type=F32).astype(BF16)
        back = jnp.concatenate([back[:n], back[n:]], 1)
        grad = jnp.dot(back, fwd_ref[...], preferred_element_type=F32)
        grad_re, grad_im = grad[:, :n], grad[:, n:]
        pterm_ref[0] += patch_re * grad_re + patch_im * grad_im
        pterm_ref[1] += patch_re * grad_im - patch_im * grad_re
        terms = (probe_re * grad_re + probe_im * grad_im, probe_re * grad_im - probe_im * grad_re)
        for k in range(2):
            if shift is None:
                grad_ref[k, :, col : col + n] += terms[k]
            else:
                padded = jnp.concatenate([terms[k], jnp.zeros((n, LANES), F32)], 1)
                grad_ref[k, :, pl.ds(base, wide)] += pltpu.roll(padded, shift, axis=1)
    core_ref[...] = grad_ref[:, HALO : HALO + rows]
    for side, start in ((0, 0), (1, HALO + rows)):
        rim = grad_ref[:, start : start + HALO].astype(BF16)
        rimw_ref[side] = rim[:, :, wlo:whi]
        rimr_ref[side] = jnp.concatenate([rim[:, :, :wlo], rim[:, :, whi:]], 2)


def frames(offsets, own, low, high, probe, amps, wlo, whi):
    nf, n, _ = amps.shape
    _, rows, width = own.shape
    fwd, inv = dft_blocks(n)
    full = lambda shape: pl.BlockSpec(shape, lambda: (0,) * len(shape))
    rim_w, rim_r = whi - wlo, width - (whi - wlo)
    ext = rows + 2 * HALO
    return pl.pallas_call(
        functools.partial(frames_kernel, wlo=wlo, whi=whi),
        in_specs=[
            pl.BlockSpec(memory_space=pltpu.SMEM),
            full(own.shape),
            full(low.shape),
            full(high.shape),
            full(probe.shape),
            full(amps.shape),
            full(fwd.shape),
            full(inv.shape),
        ],
        out_specs=[
            full(own.shape),
            full((2, 2, HALO, rim_w)),
            full((2, 2, HALO, rim_r)),
            full(probe.shape),
        ],
        out_shape=[
            jax.ShapeDtypeStruct(own.shape, F32),
            jax.ShapeDtypeStruct((2, 2, HALO, rim_w), BF16),
            jax.ShapeDtypeStruct((2, 2, HALO, rim_r), BF16),
            jax.ShapeDtypeStruct(probe.shape, F32),
        ],
        scratch_shapes=[pltpu.VMEM((2, ext, width), F32), pltpu.VMEM((2, ext, width), F32)],
        name="frames",
    )(offsets, own, low, high, probe, amps, jnp.asarray(fwd), jnp.asarray(inv))


def detector_plan(theta, width, lo, span):
    na = theta.shape[0]
    hy = NG // 2
    center = (NG - 1) / 2.0
    c, s = jnp.cos(theta), jnp.sin(theta)
    cc, ss = c[None, :, None], s[None, :, None]
    xg = jnp.arange(NG // GROUP, dtype=F32)[:, None, None] * GROUP - center
    ylo = jnp.arange(2, dtype=F32)[None, None, :] * hy - center
    first = (width - 1) / 2.0 - lo + 2.0 * (
        xg * cc
        + jnp.minimum(0.0, (GROUP - 1) * cc)
        + jnp.minimum(ylo * ss, (ylo + (hy - 1)) * ss)
    )
    start = jnp.clip(jnp.floor(first - 1.0 / 64), 0.0, span - 1.0)
    lane = jnp.arange(LANES, dtype=jnp.int32)
    side = jnp.arange(2, dtype=jnp.int32)
    xpair = jnp.arange(NG // 2, dtype=F32) * 2.0 - center
    xlane = ((lane[None, :] // hy) ^ side[:, None]).astype(F32)
    ylane = (lane[None, :] % hy).astype(F32) + (side[:, None].astype(F32) * hy - center)
    xpos = xpair[:, None, None, None] + xlane[None, None]
    upos = (width - 1) / 2.0 + 2.0 * (xpos * c[None, :, None, None] + ylane[None, None] * s[None, :, None, None])
    lower = jnp.clip(jnp.floor(upos), 0.0, width - 2.0)
    frac = upos - lower
    local = (lower - lo - jnp.repeat(start, GROUP // 2, axis=0)[..., None]).astype(jnp.int32)
    flat = NG // 2 * na * 2
    return (
        start.astype(jnp.int32).reshape(-1),
        (local & (LANES - 1)).reshape(flat, LANES),
        frac.reshape(flat, LANES),
    )


GATHER_LANES = lax.GatherDimensionNumbers(
    offset_dims=(),
    collapsed_slice_dims=(1,),
    start_index_map=(1,),
    operand_batching_dims=(0,),
    start_indices_batching_dims=(0,),
)


def lane_gather(table, index):
    return lax.gather(
        table, index[..., None], GATHER_LANES, slice_sizes=(1, 1),
        mode=lax.GatherScatterMode.PROMISE_IN_BOUNDS,
    )


def volume_kernel(start_ref, phase_ref, index_ref, frac_ref, out_ref, tab_ref, win_ref, scale_ref, *, groups):
    na, nz, span = phase_ref.shape
    nzg = nz // 8
    hy = NG // 2
    step = pl.program_id(0)
    low_half = lax.broadcasted_iota(jnp.int32, (8, LANES), 1) < hy
    lane = lax.broadcasted_iota(jnp.int32, (nz, LANES), 1)

    def windows(group, slot):
        for j in range(2 * na):
            start = start_ref[group * (2 * na) + j]
            tile = pl.multiple_of((start >> 7) * LANES, LANES)
            rest = start & (LANES - 1)
            left = pltpu.roll(tab_ref[j // 2, :, pl.ds(tile, LANES)], LANES - rest, axis=1)
            right = pltpu.roll(tab_ref[j // 2, :, pl.ds(tile + LANES, LANES)], LANES - rest, axis=1)
            win_ref[slot * 2 * na + j] = jnp.where(lane < LANES - rest, left, right)

    @pl.when(step == 0)
    def _():
        values = [phase_ref[a].astype(F32) for a in range(na)]
        peak = functools.reduce(
            jnp.maximum, [jnp.max(jnp.abs(v), axis=1, keepdims=True) for v in values]
        )
        scale = jnp.where(peak > 0, 16383.0 / peak, 0.0)
        scale_ref[...] = jnp.broadcast_to(peak * (1.0 / (16383.0 * 65536.0)), (nz, LANES))
        for a in range(na):
            q = jnp.round(values[a] * scale).astype(jnp.int32)
            d = pltpu.roll(q, span - 1, axis=1) - q
            tab_ref[a, :, 0:span] = (d << 16) + q
            tab_ref[a, :, span:] = jnp.zeros((nz, LANES), jnp.int32)
        windows(0, 0)

    def emit(slot):
        for p in range(GROUP // 2):
            sums = [[None] * nzg for _ in range(2)]
            for a in range(na):
                for side in range(2):
                    row = ((slot * (GROUP // 2) + p) * na + a) * 2 + side
                    index = jnp.broadcast_to(index_ref[row : row + 1, :], (8, LANES))
                    frac = jnp.broadcast_to(frac_ref[row : row + 1, :], (8, LANES))
                    for zg in range(nzg):
                        packed = lane_gather(win_ref[slot * 2 * na + 2 * a + side, zg * 8 : zg * 8 + 8, :], index)
                        term = (packed << 16).astype(F32) + frac * packed.astype(F32)
                        sums[side][zg] = term if a == 0 else sums[side][zg] + term
            for zg in range(nzg):
                z = slice(zg * 8, zg * 8 + 8)
                first = sums[0][zg] * scale_ref[z, :]
                second = sums[1][zg] * scale_ref[z, :]
                at = (slot * GROUP + 2 * p) * LANES
                out_ref[z, at : at + LANES] = jnp.where(low_half, first, second)
                out_ref[z, at + LANES : at + 2 * LANES] = pltpu.roll(
                    jnp.where(low_half, second, first), hy, axis=1
                )

    windows(2 * step + 1, 1)
    emit(0)
    windows(jnp.minimum(2 * step + 2, groups - 1), 0)
    emit(1)


def volume(plan, phases):
    na, nz, span = phases.shape
    start, index, frac = plan
    groups = NG // GROUP
    rows = GROUP * na * 2
    return pl.pallas_call(
        functools.partial(volume_kernel, groups=groups),
        grid=(groups // 2,),
        in_specs=[
            pl.BlockSpec(memory_space=pltpu.SMEM),
            pl.BlockSpec((na, nz, span), lambda i: (0, 0, 0)),
            pl.BlockSpec((rows, LANES), lambda i: (i, 0)),
            pl.BlockSpec((rows, LANES), lambda i: (i, 0)),
        ],
        out_specs=pl.BlockSpec((nz, 2 * GROUP * NG), lambda i: (0, i)),
        out_shape=jax.ShapeDtypeStruct((nz, NG * NG), F32),
        scratch_shapes=[
            pltpu.VMEM((na, nz, span + LANES), jnp.int32),
            pltpu.VMEM((4 * na, nz, LANES), jnp.int32),
            pltpu.VMEM((nz, LANES), F32),
        ],
        name="volume",
    )(start, phases, index, frac)


def swap(value, axis, stride):
    count = lax.axis_size(axis)
    return lax.ppermute(value, axis, [(i, i ^ stride) for i in range(count)])


def halves(value, axis, stride):
    bit = (lax.axis_index(axis) // stride) % 2
    pick = lambda at: lax.dynamic_index_in_dim(value, at, 0, keepdims=False)
    return pick(bit), pick(1 - bit), bit


def exchange_angles(value):
    stride = lax.axis_size("angle") // 2
    slots = [value]
    while stride:
        kept, sent = [], []
        for v in slots:
            mine, other, _ = halves(v.reshape((2, v.shape[0] // 2) + v.shape[1:]), "angle", stride)
            kept.append(mine)
            sent.append(other)
        got = swap(jnp.stack(sent), "angle", stride)
        slots = kept + [got[i] for i in range(len(sent))]
        stride //= 2
    count = len(slots)
    bits = count.bit_length() - 1
    order = [int(format(j, f"0{bits}b")[::-1], 2) for j in range(count)] if bits else [0]
    return jnp.stack([slots[order[j]][0] for j in range(count)])


def sum_everywhere(value):
    count = lax.axis_size("strip")
    split = [s for s in (1, 2) if s < count]
    joins = []
    for stride in split:
        if stride > 1:
            value = value.reshape((2, value.shape[0] // 2) + value.shape[1:])
        mine, other, bit = halves(value, "strip", stride)
        value = mine + swap(other.astype(BF16), "strip", stride).astype(F32)
        joins.append((stride, bit))
    stages = [("strip", 1 << k) for k in range(len(split), count.bit_length() - 1)]
    stages += [("angle", 1 << k) for k in range(lax.axis_size("angle").bit_length() - 1)]
    for axis, stride in stages:
        rounded = value.astype(BF16)
        value = rounded.astype(F32) + swap(rounded, axis, stride).astype(F32)
    value = value.astype(BF16)
    for stride, bit in joins[::-1]:
        got = swap(value, "strip", stride)
        value = jnp.where(bit == 0, jnp.stack([value, got]), jnp.stack([got, value]))
        if stride > 1:
            value = value.reshape((-1,) + value.shape[2:])
    return value.astype(F32)


def shards(object_field, amplitudes, scan_offsets, probe_field, tilt_angles):
    strip_rows = object_field.shape[2]
    width = object_field.shape[3]
    angles = lax.axis_size("angle")
    strips = lax.axis_size("strip")
    own = object_field[:, 0]
    reach = math.sqrt(2.0) * (NG - 1)
    lo = int(math.floor((width - 1) / 2.0 - reach - 1)) // HALO * HALO
    span = -(-int(math.ceil((width - 1) / 2.0 + reach + 2) - lo) // LANES) * LANES
    assert 0 <= lo and lo + span <= width and NG == LANES
    wlo = lo // LANES * LANES
    whi = -(-(lo + span) // LANES) * LANES

    forward = [(i, i + 1) for i in range(strips - 1)]
    backward = [(i + 1, i) for i in range(strips - 1)]
    rounded = own.astype(BF16)
    low = lax.ppermute(rounded[:, strip_rows - HALO :], "strip", forward)
    high = lax.ppermute(rounded[:, :HALO], "strip", backward)

    me = lax.axis_index("angle")
    theta = jnp.take(tilt_angles, me ^ jnp.arange(angles, dtype=jnp.int32))
    plan = detector_plan(theta, width, lo, span)

    core, rim_w, rim_r, probe_terms = frames(
        scan_offsets[0], own, low, high, probe_field, amplitudes[0], wlo, whi
    )
    above_w = lax.ppermute(rim_w[0], "strip", backward)
    below_w = lax.ppermute(rim_w[1], "strip", forward)
    rims_w = jnp.concatenate([below_w, above_w], 1).astype(F32)
    grad_w = core[:, :, lo : lo + span] + rims_w[:, :, lo - wlo : lo - wlo + span]
    own_w = own[:, :, lo : lo + span]
    phase = (own_w[0] * grad_w[1] - own_w[1] * grad_w[0]).astype(BF16)
    phases = exchange_angles(phase.reshape(angles, strip_rows // angles, span))
    result = volume(plan, phases)

    above_r = lax.ppermute(rim_r[0], "strip", backward)
    below_r = lax.ppermute(rim_r[1], "strip", forward)
    rims_r = jnp.concatenate([below_r, above_r], 1).astype(F32)
    rims = jnp.concatenate([rims_r[:, :, :wlo], rims_w, rims_r[:, :, wlo:]], 2)
    object_grad = (core + rims)[:, None]

    frames_all = angles * strips * scan_offsets.shape[1]
    probe_grad = sum_everywhere(probe_terms) * (1.0 / math.sqrt(frames_all))
    return object_grad, probe_grad, result[None, None]


def solution(mesh):
    return jax.shard_map(
        shards,
        mesh=mesh,
        in_specs=(
            P(None, "angle", "strip", None),
            P("angle", "strip", None, None),
            P("angle", "strip", None),
            P(),
            P(),
        ),
        out_specs=(P(None, "angle", "strip", None), P(), P("strip", "angle", None, None)),
        check_vma=False,
    )
```

```python
import functools
import math

import jax
import jax.numpy as jnp
import numpy as np
from jax import lax
from jax.experimental import pallas as pl
from jax.experimental.pallas import tpu as pltpu
from jax.sharding import PartitionSpec as P

HALO = 64
NG = 128
LANES = 128
BLOCK = 32
PARTS = 1
VMEM_LIMIT = 20 << 20
FETCH_LIMIT = 20 << 20
F32 = jnp.float32
BF16 = jnp.bfloat16


def dft_tables(size):
    k = np.arange(size)
    arg = 2.0 * np.pi / size * ((k[:, None] * k[None, :]) % size)
    tables = np.stack([np.cos(arg), np.sin(arg)]) / math.sqrt(size)
    return tables.astype(np.float32).astype(jnp.bfloat16)


def frames_kernel(col_ref, near_ref, far_ref, own_ref, probe_ref, amp_ref, tab_ref,
                  core_ref, view_ref, rnear_ref, rfar_ref, kept_ref, sent_ref, ext_ref, grad_ref, pterm_ref, fwd_ref, inv_ref, *, wlo, whi):
    nf, n, _ = amp_ref.shape
    rows = own_ref.shape[1]
    width = own_ref.shape[2]
    wide = n + LANES
    odd = lax.axis_index("strip") % 2
    below = HALO + rows
    near_row = pl.multiple_of(jnp.where(odd == 0, below, 0), HALO)
    far_row = pl.multiple_of(jnp.where(odd == 0, 0, below), HALO)
    ext_ref[:, HALO:below] = own_ref[...]
    cos, sin = tab_ref[0], tab_ref[1]
    fwd_ref[:n, :n] = cos
    fwd_ref[:n, n:] = sin
    fwd_ref[n:, :n] = -sin
    fwd_ref[n:, n:] = cos
    inv_ref[:n, :n] = cos
    inv_ref[:n, n:] = -sin
    inv_ref[n:, :n] = sin
    inv_ref[n:, n:] = cos
    grad_ref[...] = jnp.zeros_like(grad_ref)
    pterm_ref[...] = jnp.zeros_like(pterm_ref)
    ext_ref[:, pl.ds(near_row, HALO)] = near_ref[...].astype(F32)
    ext_ref[:, pl.ds(far_row, HALO)] = far_ref[...].astype(F32)
    static_cols = (width - n, 0, (width - n) // 2)
    for f in range(nf):
        if f < 3 and static_cols[f] % LANES == 0:
            col, shift = static_cols[f], None
            patch_re = ext_ref[0, :, col : col + n]
            patch_im = ext_ref[1, :, col : col + n]
        else:
            at = col_ref[f]
            base = pl.multiple_of(jnp.minimum((at >> 7) * LANES, width - wide), LANES)
            shift = at - base
            patch_re = pltpu.roll(ext_ref[0, :, pl.ds(base, wide)], wide - shift, axis=1)[:, :n]
            patch_im = pltpu.roll(ext_ref[1, :, pl.ds(base, wide)], wide - shift, axis=1)[:, :n]
        probe_re, probe_im = probe_ref[0], probe_ref[1]
        exit_wave = jnp.concatenate(
            [probe_re * patch_re - probe_im * patch_im, probe_re * patch_im + probe_im * patch_re], 0
        ).astype(BF16)
        half = jnp.dot(fwd_ref[...], exit_wave, preferred_element_type=F32).astype(BF16)
        half = jnp.concatenate([half[:n], half[n:]], 1)
        wave = jnp.dot(half, inv_ref[...], preferred_element_type=F32)
        wave_re, wave_im = wave[:, :n], wave[:, n:]
        factor = 1.0 - amp_ref[f].astype(F32) * lax.rsqrt(wave_re * wave_re + wave_im * wave_im + 1.0)
        misfit = jnp.concatenate([wave_re * factor, wave_im * factor], 0).astype(BF16)
        back = jnp.dot(inv_ref[...], misfit, preferred_element_type=F32).astype(BF16)
        back = jnp.concatenate([back[:n], back[n:]], 1)
        grad = jnp.dot(back, fwd_ref[...], preferred_element_type=F32)
        grad_re, grad_im = grad[:, :n], grad[:, n:]
        pterm_ref[0] += patch_re * grad_re + patch_im * grad_im
        pterm_ref[1] += patch_re * grad_im - patch_im * grad_re
        terms = (probe_re * grad_re + probe_im * grad_im, probe_re * grad_im - probe_im * grad_re)
        for k in range(2):
            if shift is None:
                grad_ref[k, :, col : col + n] += terms[k]
            else:
                padded = jnp.concatenate([terms[k], jnp.zeros((n, LANES), F32)], 1)
                grad_ref[k, :, pl.ds(base, wide)] += pltpu.roll(padded, shift, axis=1)

    sent_ref[...] = pterm_ref[1 - odd].astype(BF16)
    kept_ref[...] = pterm_ref[odd]
    rnear_ref[...] = grad_ref[:, pl.ds(near_row, HALO)].astype(BF16)
    rfar_ref[...] = grad_ref[:, pl.ds(far_row, HALO)].astype(BF16)
    core_ref[...] = grad_ref[:, HALO:below]
    view_ref[...] = own_ref[:, :, wlo:whi]


def in_vmem(count):
    return [pl.BlockSpec(memory_space=pltpu.VMEM)] * count


def fetch_kernel(*refs):
    sems = refs[-1]
    count = (len(refs) - 1) // 2
    copies = [pltpu.make_async_copy(refs[k], refs[count + k], sems.at[k]) for k in range(count)]
    for copy in copies:
        copy.start()
    for copy in copies:
        copy.wait()


def fetch(*arrays):
    size = sum(x.size * x.dtype.itemsize for x in arrays)
    return pl.pallas_call(
        fetch_kernel,
        in_specs=[pl.BlockSpec(memory_space=pltpu.HBM)] * len(arrays),
        out_specs=in_vmem(len(arrays)),
        out_shape=[jax.ShapeDtypeStruct(x.shape, x.dtype) for x in arrays],
        scratch_shapes=[pltpu.SemaphoreType.DMA((len(arrays),))],
        compiler_params=pltpu.CompilerParams(vmem_limit_bytes=FETCH_LIMIT),
        cost_estimate=pl.CostEstimate(flops=0, bytes_accessed=size, transcendentals=0),
        name="fetch",
    )(*arrays)


def frames(columns, near, far, own, probe, amps, tables, wlo, whi):
    nf, n, _ = amps.shape
    _, rows, width = own.shape
    ext = rows + 2 * HALO
    assert ext == n and rows == 2 * HALO
    args = (near, far, own, probe, amps, tables)
    outs = [
        jax.ShapeDtypeStruct(own.shape, F32),
        jax.ShapeDtypeStruct((2, rows, whi - wlo), F32),
        jax.ShapeDtypeStruct((2, HALO, width), BF16),
        jax.ShapeDtypeStruct((2, HALO, width), BF16),
        jax.ShapeDtypeStruct((n, n), F32),
        jax.ShapeDtypeStruct((n, n), BF16),
    ]
    return pl.pallas_call(
        functools.partial(frames_kernel, wlo=wlo, whi=whi),
        in_specs=[pl.BlockSpec(memory_space=pltpu.SMEM)] + in_vmem(6),
        out_specs=in_vmem(len(outs)),
        out_shape=outs,
        scratch_shapes=[
            pltpu.VMEM((2, ext, width), F32),
            pltpu.VMEM((2, ext, width), F32),
            pltpu.VMEM((2, n, n), F32),
            pltpu.VMEM((2 * n, 2 * n), BF16),
            pltpu.VMEM((2 * n, 2 * n), BF16),
        ],
        compiler_params=pltpu.CompilerParams(vmem_limit_bytes=VMEM_LIMIT),
        cost_estimate=pl.CostEstimate(flops=64 * nf * n**3, bytes_accessed=6 << 20, transcendentals=nf * n * n),
        name="frames",
    )(columns, *args)


def phase_kernel(view_ref, core_ref, near_ref, far_ref, phase_ref, *, lo, wlo, whi):
    rows = view_ref.shape[1]
    span = phase_ref.shape[1]
    odd = lax.axis_index("strip") % 2
    for rim_ref, parity in ((near_ref, odd), (far_ref, 1 - odd)):
        at = pl.ds(pl.multiple_of(jnp.where(parity == 0, rows - HALO, 0), HALO), HALO)
        grad_re = core_ref[0, at, wlo:whi] + rim_ref[0, :, wlo:whi].astype(F32)
        grad_im = core_ref[1, at, wlo:whi] + rim_ref[1, :, wlo:whi].astype(F32)
        phase = view_ref[0, at] * grad_im - view_ref[1, at] * grad_re
        if lo > wlo:
            phase = pltpu.roll(phase, whi - lo, axis=1)
        phase_ref[at] = phase[:, :span].astype(BF16)


def merged_phase(view, core, near, far, lo, span, wlo, whi):
    return pl.pallas_call(
        functools.partial(phase_kernel, lo=lo, wlo=wlo, whi=whi),
        in_specs=in_vmem(4),
        out_specs=pl.BlockSpec(memory_space=pltpu.VMEM),
        out_shape=jax.ShapeDtypeStruct((view.shape[1], span), BF16),
        compiler_params=pltpu.CompilerParams(vmem_limit_bytes=VMEM_LIMIT),
        cost_estimate=pl.CostEstimate(flops=1 << 19, bytes_accessed=1 << 20, transcendentals=0),
        name="phase",
    )(view, core, near, far)


def rim_kernel(core_ref, near_ref, far_ref, grad_ref):
    rows = core_ref.shape[1]
    odd = lax.axis_index("strip") % 2
    for rim_ref, parity in ((near_ref, odd), (far_ref, 1 - odd)):
        at = pl.ds(pl.multiple_of(jnp.where(parity == 0, rows - HALO, 0), HALO), HALO)
        grad_ref[:, at] = core_ref[:, at] + rim_ref[...].astype(F32)


def merged_grad(core, near, far):
    return pl.pallas_call(
        rim_kernel,
        in_specs=in_vmem(3),
        out_specs=pl.BlockSpec(memory_space=pltpu.VMEM),
        out_shape=jax.ShapeDtypeStruct(core.shape, F32),
        compiler_params=pltpu.CompilerParams(vmem_limit_bytes=VMEM_LIMIT),
        cost_estimate=pl.CostEstimate(flops=1 << 18, bytes_accessed=2 << 20, transcendentals=0),
        name="rims",
    )(core, near, far)


def fold_kernel(kept_ref, got_ref, mine_ref, other_ref):
    rows = mine_ref.shape[0]
    bit = lax.axis_index("angle") % 2
    for out_ref, which in ((other_ref, 1 - bit), (mine_ref, bit)):
        at = pl.ds(pl.multiple_of(which * rows, rows), rows)
        out_ref[...] = (kept_ref[at] + got_ref[at].astype(F32)).astype(out_ref.dtype)


def fold(kept, got):
    shape = (kept.shape[0] // 2, kept.shape[1])
    return pl.pallas_call(
        fold_kernel,
        in_specs=in_vmem(2),
        out_specs=in_vmem(2),
        out_shape=[jax.ShapeDtypeStruct(shape, F32), jax.ShapeDtypeStruct(shape, BF16)],
        compiler_params=pltpu.CompilerParams(vmem_limit_bytes=VMEM_LIMIT),
        cost_estimate=pl.CostEstimate(flops=kept.size, bytes_accessed=8 * kept.size, transcendentals=0),
        name="fold",
    )(kept, got)


def detector_plan(theta, width, lo, span):
    center = (NG - 1) / 2.0
    n = NG // BLOCK
    c = jnp.cos(theta)[None, None, :]
    s = jnp.sin(theta)[None, None, :]
    x0 = (jnp.arange(n, dtype=F32) * BLOCK - center)[:, None, None]
    y0 = (jnp.arange(n, dtype=F32) * BLOCK - center)[None, :, None]
    first = (width - 1) / 2.0 - lo + 2.0 * (
        x0 * c + jnp.minimum(0.0, (BLOCK - 1) * c) + y0 * s + jnp.minimum(0.0, (BLOCK - 1) * s)
    )
    base = jnp.clip(jnp.floor((first - 1.0 / 64) / BLOCK), 0, span // BLOCK - 1) * BLOCK
    sub = jnp.arange(8, dtype=jnp.int32)[:, None]
    lane = jnp.arange(LANES, dtype=jnp.int32)[None, :]
    yblock = jnp.arange(n, dtype=jnp.int32)[:, None, None]
    xin = ((lane // BLOCK - yblock) % n * 8 + sub[None]).astype(F32)
    yin = (lane % BLOCK).astype(F32)[None]
    xpos = x0[:, :, :, None, None] + xin[None, :, None]
    ypos = y0[:, :, :, None, None] + yin[None, :, None]
    upos = (width - 1) / 2.0 + 2.0 * (xpos * c[..., None, None] + ypos * s[..., None, None])
    lower = jnp.clip(jnp.floor(upos), 0.0, width - 2.0)
    frac = upos - lower
    local = (lower - lo - base[..., None, None]).astype(jnp.int32) & (LANES - 1)
    flat = n * n * theta.shape[0] * 8
    return base.astype(jnp.int32).reshape(-1), local.reshape(flat, LANES), frac.reshape(flat, LANES)


GATHER_LANES = lax.GatherDimensionNumbers(
    offset_dims=(),
    collapsed_slice_dims=(1,),
    start_index_map=(1,),
    operand_batching_dims=(0,),
    start_indices_batching_dims=(0,),
)


def lane_gather(table, index):
    return lax.gather(
        table, index[..., None], GATHER_LANES, slice_sizes=(1, 1),
        mode=lax.GatherScatterMode.PROMISE_IN_BOUNDS,
    )


def volume_kernel(base_ref, phase_ref, index_ref, frac_ref, *refs, begin):
    out_ref, tab_ref, scale_ref, part_ref = refs[-4:]
    na, nz, span = phase_ref.shape
    n = NG // BLOCK
    top = float(32767 // na)
    zc = min(16, nz)
    step = pl.program_id(0)

    @pl.when(step == 0)
    def _():
        values = [phase_ref[a].astype(F32) for a in range(na)]
        peak = functools.reduce(
            jnp.maximum, [jnp.max(jnp.abs(v), axis=1, keepdims=True) for v in values]
        )
        scale = jnp.where(peak > 0, top / peak, 0.0)
        scale_ref[...] = jnp.broadcast_to(peak * (1.0 / (top * 65536.0)), (nz, LANES))
        for a in range(na):
            q = jnp.round(values[a] * scale).astype(jnp.int32)
            packed = ((pltpu.roll(q, span - 1, axis=1) - q) << 16) + q
            for k in range(n):
                tab_ref[a * n + k] = packed if k == 0 else pltpu.roll(packed, span - BLOCK * k, axis=1)

    for z0 in range(0, nz, zc):
        for yb in range(n):
            sums = [None] * zc
            for a in range(na):
                base = base_ref[((begin + step) * n + yb) * na + a]
                copy = a * n + (base // BLOCK) % n
                tile = pl.multiple_of(base // LANES * LANES, LANES)
                row = (yb * na + a) * 8
                index = index_ref[row : row + 8, :]
                frac = frac_ref[row : row + 8, :]
                for i in range(zc):
                    line = tab_ref[copy, z0 + i : z0 + i + 1, pl.ds(tile, LANES)]
                    packed = lane_gather(jnp.broadcast_to(line, (8, LANES)), index)
                    slope = frac * packed.astype(F32)
                    sums[i] = (packed, slope) if a == 0 else (sums[i][0] + packed, sums[i][1] + slope)
            for i in range(zc):
                part_ref[yb, z0 + i] = (sums[i][0] << 16).astype(F32) + sums[i][1]
    flat = out_ref.reshape(nz * BLOCK, LANES)
    block = lax.broadcasted_iota(jnp.int32, (8, LANES), 1) // BLOCK
    for z in range(nz):
        parts = [part_ref[yb, z] for yb in range(n)]
        scale = jnp.broadcast_to(scale_ref[z : z + 1, :], (8, LANES))
        for k in range(n):
            line = parts[-k % n]
            for p in range(1, n):
                line = jnp.where(block == p, parts[(p - k) % n], line)
            line = line * scale
            if k:
                line = pltpu.roll(line, LANES - BLOCK * k, axis=1)
            flat[pl.ds(((z // 8) * BLOCK + k * 8) * 8 + z % 8, 8, stride=8), :] = line


def volume(plan, phases, begin, count, previous=None):
    na, nz, span = phases.shape
    base, index, frac = plan
    n = NG // BLOCK
    rows = n * na * 8
    steps = lambda i: (i + begin, 0)
    specs = [
        pl.BlockSpec(memory_space=pltpu.SMEM),
        pl.BlockSpec((na, nz, span), lambda i: (0, 0, 0)),
        pl.BlockSpec((rows, LANES), steps),
        pl.BlockSpec((rows, LANES), steps),
    ]
    args = [base, phases, index, frac]
    alias = {}
    if previous is not None:
        specs.append(pl.BlockSpec(memory_space=pl.ANY))
        args.append(previous)
        alias = {4: 0}
    return pl.pallas_call(
        functools.partial(volume_kernel, begin=begin),
        grid=(count,),
        in_specs=specs,
        out_specs=pl.BlockSpec((nz // 8, BLOCK, 8, LANES), lambda i: (0, i + begin, 0, 0)),
        out_shape=jax.ShapeDtypeStruct((nz // 8, NG, 8, LANES), F32),
        input_output_aliases=alias,
        scratch_shapes=[
            pltpu.VMEM((na * n, nz, span), jnp.int32),
            pltpu.VMEM((nz, LANES), F32),
            pltpu.VMEM((n, nz, 8, LANES), F32),
        ],
        compiler_params=pltpu.CompilerParams(vmem_limit_bytes=VMEM_LIMIT),
        cost_estimate=pl.CostEstimate(flops=count << 25, bytes_accessed=count << 21, transcendentals=0),
    )(*args)


def swap(value, axis, stride):
    count = lax.axis_size(axis)
    return lax.ppermute(value, axis, [(i, i ^ stride) for i in range(count)])


def halves(value, axis, stride):
    bit = (lax.axis_index(axis) // stride) % 2
    pick = lambda at: lax.dynamic_index_in_dim(value, at, 0, keepdims=False)
    return pick(bit), pick(1 - bit), bit


def exchange_angles(value):
    stride = lax.axis_size("angle") // 2
    slots = [value]
    while stride:
        kept, sent = [], []
        for v in slots:
            mine, other, _ = halves(v.reshape((2, v.shape[0] // 2) + v.shape[1:]), "angle", stride)
            kept.append(mine)
            sent.append(other)
        got = swap(jnp.stack(sent), "angle", stride)
        slots = kept + [got[i] for i in range(len(sent))]
        stride //= 2
    bits = len(slots).bit_length() - 1
    order = [int(format(j, f"0{bits}b")[::-1], 2) for j in range(len(slots))]
    return jnp.stack([slots[j][0] for j in order])


def sum_everywhere(kept, sent):
    mine, other = fold(kept, swap(sent, "strip", 1))
    value = mine + swap(other, "angle", 1).astype(F32)
    stages = [("angle", 1 << k) for k in range(1, lax.axis_size("angle").bit_length() - 1)]
    stages += [("strip", 1 << k) for k in range(1, lax.axis_size("strip").bit_length() - 1)]
    for axis, stride in stages:
        rounded = value.astype(BF16)
        value = rounded.astype(F32) + swap(rounded, axis, stride).astype(F32)
    value = value.astype(BF16)
    for axis, stride in (("angle", 1), ("strip", 1)):
        got = swap(value, axis, stride)
        bit = lax.axis_index(axis) % 2
        value = jnp.where(bit == 0, jnp.stack([value, got]), jnp.stack([got, value]))
        if axis == "angle":
            value = value.reshape((-1,) + value.shape[2:])
    return value.astype(F32)


def shards(object_field, amplitudes, scan_offsets, probe_field, tilt_angles):
    strip_rows = object_field.shape[2]
    width = object_field.shape[3]
    angles = lax.axis_size("angle")
    strips = lax.axis_size("strip")
    assert strips % 2 == 0 and strips & (strips - 1) == 0 and angles & (angles - 1) == 0 and angles > 1
    reach = math.sqrt(2.0) * (NG - 1)
    lo = int(math.floor((width - 1) / 2.0 - reach - 1)) // HALO * HALO
    span = -(-int(math.ceil((width - 1) / 2.0 + reach + 2) - lo) // LANES) * LANES
    assert 0 <= lo and lo + span <= width and NG == LANES
    wlo = lo // LANES * LANES
    whi = -(-(lo + span) // LANES) * LANES

    beside = [(i, i + 1 if i % 2 else i - 1) for i in range(1, strips - 1)]

    def far_swap(value):
        return lax.ppermute(value, "strip", beside)

    own = object_field[:, 0]
    odd = lax.axis_index("strip") % 2
    half = lambda at: lax.dynamic_slice_in_dim(own, at * HALO, HALO, 1).astype(BF16)
    far, near, *inputs = lax.optimization_barrier(
        (half(odd), half(1 - odd), own, probe_field, amplitudes[0])
    )
    far = far_swap(far)
    near = swap(near, "strip", 1)

    me = lax.axis_index("angle")
    theta = jnp.take(tilt_angles, me ^ jnp.arange(angles, dtype=jnp.int32))
    plan = detector_plan(theta, width, lo, span)

    tables = jnp.asarray(dft_tables(amplitudes.shape[2]))
    inputs, plan, columns = lax.optimization_barrier((inputs, plan, scan_offsets[0, :, 1]))
    inputs = fetch(*inputs, tables)
    core, view, rnear, rfar, kept, sent = frames(columns, near, far, *inputs, wlo, whi)
    rfar = far_swap(rfar)
    rnear = swap(rnear, "strip", 1)
    phase = merged_phase(view, core, rnear, rfar, lo, span, wlo, whi)
    object_grad = merged_grad(core, rnear, rfar)
    phases = exchange_angles(phase.reshape(angles, strip_rows // angles, span))
    blocks = NG // BLOCK
    result = None
    for part in range(PARTS):
        result = volume(plan, phases, part * blocks // PARTS, blocks // PARTS, result)
    slices = strip_rows // angles
    result = result.transpose(0, 2, 1, 3).reshape(1, 1, slices, NG * NG)

    frames_all = angles * strips * scan_offsets.shape[1]
    probe_grad = sum_everywhere(kept, sent) * (1.0 / math.sqrt(frames_all))
    return object_grad[:, None], probe_grad, result


def solution(mesh):
    return jax.shard_map(
        shards,
        mesh=mesh,
        in_specs=(
            P(None, "angle", "strip", None),
            P("angle", "strip", None, None),
            P("angle", "strip", None),
            P(),
            P(),
        ),
        out_specs=(P(None, "angle", "strip", None), P(), P("strip", "angle", None, None)),
        check_vma=False,
    )
```

```python
import functools
import math

import jax
import jax.numpy as jnp
import numpy as np
from jax import lax
from jax.experimental import pallas as pl
from jax.experimental.pallas import tpu as pltpu
from jax.sharding import PartitionSpec as P

HALO = 64
NG = 128
LANES = 128
BLOCK = 32
PARTS = 2
VMEM_LIMIT = 20 << 20
FETCH_LIMIT = 20 << 20
F32 = jnp.float32
BF16 = jnp.bfloat16


def dft_tables(size):
    k = np.arange(size)
    arg = 2.0 * np.pi / size * ((k[:, None] * k[None, :]) % size)
    tables = np.stack([np.cos(arg), np.sin(arg)]) / math.sqrt(size)
    return tables.astype(np.float32).astype(jnp.bfloat16)


def frames_kernel(col_ref, near_ref, far_ref, own_ref, probe_ref, amp_ref, tab_ref,
                  core_ref, rnear_ref, rfar_ref, kept_ref, sent_ref, ext_ref, grad_ref, pterm_ref, fwd_ref, inv_ref, *, wlo, whi):
    nf, n, _ = amp_ref.shape
    rows = own_ref.shape[1]
    width = own_ref.shape[2]
    wide = n + LANES
    odd = lax.axis_index("strip") % 2
    below = HALO + rows
    near_row = pl.multiple_of(jnp.where(odd == 0, below, 0), HALO)
    far_row = pl.multiple_of(jnp.where(odd == 0, 0, below), HALO)
    ext_ref[:, HALO:below] = own_ref[...]
    cos, sin = tab_ref[0], tab_ref[1]
    fwd_ref[:n, :n] = cos
    fwd_ref[:n, n:] = sin
    fwd_ref[n:, :n] = -sin
    fwd_ref[n:, n:] = cos
    inv_ref[:n, :n] = cos
    inv_ref[:n, n:] = -sin
    inv_ref[n:, :n] = sin
    inv_ref[n:, n:] = cos
    grad_ref[...] = jnp.zeros_like(grad_ref)
    pterm_ref[...] = jnp.zeros_like(pterm_ref)
    ext_ref[:, pl.ds(near_row, HALO)] = near_ref[...].astype(F32)
    ext_ref[:, pl.ds(far_row, HALO)] = far_ref[...].astype(F32)
    static_cols = (width - n, 0, (width - n) // 2)
    for f in range(nf):
        if f < 3 and static_cols[f] % LANES == 0:
            col, shift = static_cols[f], None
            patch_re = ext_ref[0, :, col : col + n]
            patch_im = ext_ref[1, :, col : col + n]
        else:
            at = col_ref[f]
            base = pl.multiple_of(jnp.minimum((at >> 7) * LANES, width - wide), LANES)
            shift = at - base
            patch_re = pltpu.roll(ext_ref[0, :, pl.ds(base, wide)], wide - shift, axis=1)[:, :n]
            patch_im = pltpu.roll(ext_ref[1, :, pl.ds(base, wide)], wide - shift, axis=1)[:, :n]
        probe_re, probe_im = probe_ref[0], probe_ref[1]
        exit_wave = jnp.concatenate(
            [probe_re * patch_re - probe_im * patch_im, probe_re * patch_im + probe_im * patch_re], 0
        ).astype(BF16)
        half = jnp.dot(fwd_ref[...], exit_wave, preferred_element_type=F32).astype(BF16)
        half = jnp.concatenate([half[:n], half[n:]], 1)
        wave = jnp.dot(half, inv_ref[...], preferred_element_type=F32)
        wave_re, wave_im = wave[:, :n], wave[:, n:]
        factor = 1.0 - amp_ref[f].astype(F32) * lax.rsqrt(wave_re * wave_re + wave_im * wave_im + 1.0)
        misfit = jnp.concatenate([wave_re * factor, wave_im * factor], 0).astype(BF16)
        back = jnp.dot(inv_ref[...], misfit, preferred_element_type=F32).astype(BF16)
        back = jnp.concatenate([back[:n], back[n:]], 1)
        grad = jnp.dot(back, fwd_ref[...], preferred_element_type=F32)
        grad_re, grad_im = grad[:, :n], grad[:, n:]
        pterm_ref[0] += patch_re * grad_re + patch_im * grad_im
        pterm_ref[1] += patch_re * grad_im - patch_im * grad_re
        terms = (probe_re * grad_re + probe_im * grad_im, probe_re * grad_im - probe_im * grad_re)
        for k in range(2):
            if shift is None:
                grad_ref[k, :, col : col + n] += terms[k]
            else:
                padded = jnp.concatenate([terms[k], jnp.zeros((n, LANES), F32)], 1)
                grad_ref[k, :, pl.ds(base, wide)] += pltpu.roll(padded, shift, axis=1)

    sent_ref[...] = pterm_ref[1 - odd].astype(BF16)
    kept_ref[...] = pterm_ref[odd]
    rnear_ref[...] = grad_ref[:, pl.ds(near_row, HALO)].astype(BF16)
    rfar_ref[...] = grad_ref[:, pl.ds(far_row, HALO)].astype(BF16)
    core_ref[...] = grad_ref[:, HALO:below]


def in_vmem(count):
    return [pl.BlockSpec(memory_space=pltpu.VMEM)] * count


def fetch_kernel(*refs):
    sems = refs[-1]
    count = (len(refs) - 1) // 2
    copies = [pltpu.make_async_copy(refs[k], refs[count + k], sems.at[k]) for k in range(count)]
    for copy in copies:
        copy.start()
    for copy in copies:
        copy.wait()


def fetch(*arrays):
    size = sum(x.size * x.dtype.itemsize for x in arrays)
    return pl.pallas_call(
        fetch_kernel,
        in_specs=[pl.BlockSpec(memory_space=pltpu.HBM)] * len(arrays),
        out_specs=in_vmem(len(arrays)),
        out_shape=[jax.ShapeDtypeStruct(x.shape, x.dtype) for x in arrays],
        scratch_shapes=[pltpu.SemaphoreType.DMA((len(arrays),))],
        compiler_params=pltpu.CompilerParams(vmem_limit_bytes=FETCH_LIMIT),
        cost_estimate=pl.CostEstimate(flops=0, bytes_accessed=size, transcendentals=0),
        name="fetch",
    )(*arrays)


def frames(columns, near, far, own, probe, amps, tables, wlo, whi):
    nf, n, _ = amps.shape
    _, rows, width = own.shape
    ext = rows + 2 * HALO
    assert ext == n and rows == 2 * HALO
    args = (near, far, own, probe, amps, tables)
    outs = [
        jax.ShapeDtypeStruct(own.shape, F32),
        jax.ShapeDtypeStruct((2, HALO, width), BF16),
        jax.ShapeDtypeStruct((2, HALO, width), BF16),
        jax.ShapeDtypeStruct((n, n), F32),
        jax.ShapeDtypeStruct((n, n), BF16),
    ]
    return pl.pallas_call(
        functools.partial(frames_kernel, wlo=wlo, whi=whi),
        in_specs=[pl.BlockSpec(memory_space=pltpu.SMEM)] + in_vmem(6),
        out_specs=in_vmem(len(outs)),
        out_shape=outs,
        scratch_shapes=[
            pltpu.VMEM((2, ext, width), F32),
            pltpu.VMEM((2, ext, width), F32),
            pltpu.VMEM((2, n, n), F32),
            pltpu.VMEM((2 * n, 2 * n), BF16),
            pltpu.VMEM((2 * n, 2 * n), BF16),
        ],
        compiler_params=pltpu.CompilerParams(vmem_limit_bytes=VMEM_LIMIT),
        cost_estimate=pl.CostEstimate(flops=64 * nf * n**3, bytes_accessed=6 << 20, transcendentals=nf * n * n),
        name="frames",
    )(columns, *args)


def phase_kernel(view_ref, core_ref, near_ref, far_ref, phase_ref, *, lo, wlo, whi):
    rows = view_ref.shape[1]
    span = phase_ref.shape[1]
    odd = lax.axis_index("strip") % 2
    for rim_ref, parity in ((near_ref, odd), (far_ref, 1 - odd)):
        at = pl.ds(pl.multiple_of(jnp.where(parity == 0, rows - HALO, 0), HALO), HALO)
        grad_re = core_ref[0, at, wlo:whi] + rim_ref[0, :, wlo:whi].astype(F32)
        grad_im = core_ref[1, at, wlo:whi] + rim_ref[1, :, wlo:whi].astype(F32)
        phase = view_ref[0, at, wlo:whi] * grad_im - view_ref[1, at, wlo:whi] * grad_re
        if lo > wlo:
            phase = pltpu.roll(phase, whi - lo, axis=1)
        phase_ref[at] = phase[:, :span].astype(BF16)


def merged_phase(view, core, near, far, lo, span, wlo, whi):
    return pl.pallas_call(
        functools.partial(phase_kernel, lo=lo, wlo=wlo, whi=whi),
        in_specs=in_vmem(4),
        out_specs=pl.BlockSpec(memory_space=pltpu.VMEM),
        out_shape=jax.ShapeDtypeStruct((view.shape[1], span), BF16),
        compiler_params=pltpu.CompilerParams(vmem_limit_bytes=VMEM_LIMIT),
        cost_estimate=pl.CostEstimate(flops=1 << 19, bytes_accessed=1 << 20, transcendentals=0),
        name="phase",
    )(view, core, near, far)


def rim_kernel(core_ref, near_ref, far_ref, grad_ref):
    rows = core_ref.shape[1]
    odd = lax.axis_index("strip") % 2
    for rim_ref, parity in ((near_ref, odd), (far_ref, 1 - odd)):
        at = pl.ds(pl.multiple_of(jnp.where(parity == 0, rows - HALO, 0), HALO), HALO)
        grad_ref[:, at] = core_ref[:, at] + rim_ref[...].astype(F32)


def merged_grad(core, near, far):
    return pl.pallas_call(
        rim_kernel,
        in_specs=in_vmem(3),
        out_specs=pl.BlockSpec(memory_space=pltpu.VMEM),
        out_shape=jax.ShapeDtypeStruct(core.shape, F32),
        compiler_params=pltpu.CompilerParams(vmem_limit_bytes=VMEM_LIMIT),
        cost_estimate=pl.CostEstimate(flops=1 << 18, bytes_accessed=2 << 20, transcendentals=0),
        name="rims",
    )(core, near, far)


def fold_kernel(kept_ref, got_ref, mine_ref, other_ref):
    rows = mine_ref.shape[0]
    bit = lax.axis_index("angle") % 2
    for out_ref, which in ((other_ref, 1 - bit), (mine_ref, bit)):
        at = pl.ds(pl.multiple_of(which * rows, rows), rows)
        out_ref[...] = (kept_ref[at] + got_ref[at].astype(F32)).astype(out_ref.dtype)


def fold(kept, got):
    shape = (kept.shape[0] // 2, kept.shape[1])
    return pl.pallas_call(
        fold_kernel,
        in_specs=in_vmem(2),
        out_specs=in_vmem(2),
        out_shape=[jax.ShapeDtypeStruct(shape, F32), jax.ShapeDtypeStruct(shape, BF16)],
        compiler_params=pltpu.CompilerParams(vmem_limit_bytes=VMEM_LIMIT),
        cost_estimate=pl.CostEstimate(flops=kept.size, bytes_accessed=8 * kept.size, transcendentals=0),
        name="fold",
    )(kept, got)


def detector_plan(theta, width, lo, span):
    center = (NG - 1) / 2.0
    n = NG // BLOCK
    c = jnp.cos(theta)[None, None, :]
    s = jnp.sin(theta)[None, None, :]
    x0 = (jnp.arange(n, dtype=F32) * BLOCK - center)[:, None, None]
    y0 = (jnp.arange(n, dtype=F32) * BLOCK - center)[None, :, None]
    first = (width - 1) / 2.0 - lo + 2.0 * (
        x0 * c + jnp.minimum(0.0, (BLOCK - 1) * c) + y0 * s + jnp.minimum(0.0, (BLOCK - 1) * s)
    )
    base = jnp.clip(jnp.floor((first - 1.0 / 64) / BLOCK), 0, span // BLOCK - 1) * BLOCK
    sub = jnp.arange(8, dtype=jnp.int32)[:, None]
    lane = jnp.arange(LANES, dtype=jnp.int32)[None, :]
    yblock = jnp.arange(n, dtype=jnp.int32)[:, None, None]
    xin = ((lane // BLOCK - yblock) % n * 8 + sub[None]).astype(F32)
    yin = (lane % BLOCK).astype(F32)[None]
    xpos = x0[:, :, :, None, None] + xin[None, :, None]
    ypos = y0[:, :, :, None, None] + yin[None, :, None]
    upos = (width - 1) / 2.0 + 2.0 * (xpos * c[..., None, None] + ypos * s[..., None, None])
    lower = jnp.clip(jnp.floor(upos), 0.0, width - 2.0)
    frac = upos - lower
    local = (lower - lo - base[..., None, None]).astype(jnp.int32) & (LANES - 1)
    flat = n * n * theta.shape[0] * 8
    return base.astype(jnp.int32).reshape(-1), local.reshape(flat, LANES), frac.reshape(flat, LANES)


GATHER_LANES = lax.GatherDimensionNumbers(
    offset_dims=(),
    collapsed_slice_dims=(1,),
    start_index_map=(1,),
    operand_batching_dims=(0,),
    start_indices_batching_dims=(0,),
)


def lane_gather(table, index):
    return lax.gather(
        table, index[..., None], GATHER_LANES, slice_sizes=(1, 1),
        mode=lax.GatherScatterMode.PROMISE_IN_BOUNDS,
    )


def volume_kernel(base_ref, phase_ref, index_ref, frac_ref, *refs, begin):
    out_ref, tab_ref, scale_ref, part_ref = refs[-4:]
    na, nz, span = phase_ref.shape
    n = NG // BLOCK
    top = float(32767 // na)
    zc = min(16, nz)
    step = pl.program_id(0)

    @pl.when(step == 0)
    def _():
        values = [phase_ref[a].astype(F32) for a in range(na)]
        peak = functools.reduce(
            jnp.maximum, [jnp.max(jnp.abs(v), axis=1, keepdims=True) for v in values]
        )
        scale = jnp.where(peak > 0, top / peak, 0.0)
        scale_ref[...] = jnp.broadcast_to(peak * (1.0 / (top * 65536.0)), (nz, LANES))
        for a in range(na):
            q = jnp.round(values[a] * scale).astype(jnp.int32)
            packed = ((pltpu.roll(q, span - 1, axis=1) - q) << 16) + q
            for k in range(n):
                tab_ref[a * n + k] = packed if k == 0 else pltpu.roll(packed, span - BLOCK * k, axis=1)

    for z0 in range(0, nz, zc):
        for yb in range(n):
            sums = [None] * zc
            for a in range(na):
                base = base_ref[((begin + step) * n + yb) * na + a]
                copy = a * n + (base // BLOCK) % n
                tile = pl.multiple_of(base // LANES * LANES, LANES)
                row = (yb * na + a) * 8
                index = index_ref[row : row + 8, :]
                frac = frac_ref[row : row + 8, :]
                for i in range(zc):
                    line = tab_ref[copy, z0 + i : z0 + i + 1, pl.ds(tile, LANES)]
                    packed = lane_gather(jnp.broadcast_to(line, (8, LANES)), index)
                    slope = frac * packed.astype(F32)
                    sums[i] = (packed, slope) if a == 0 else (sums[i][0] + packed, sums[i][1] + slope)
            for i in range(zc):
                part_ref[yb, z0 + i] = (sums[i][0] << 16).astype(F32) + sums[i][1]
    flat = out_ref.reshape(nz * BLOCK, LANES)
    block = lax.broadcasted_iota(jnp.int32, (8, LANES), 1) // BLOCK
    for z in range(nz):
        parts = [part_ref[yb, z] for yb in range(n)]
        scale = jnp.broadcast_to(scale_ref[z : z + 1, :], (8, LANES))
        for k in range(n):
            line = parts[-k % n]
            for p in range(1, n):
                line = jnp.where(block == p, parts[(p - k) % n], line)
            line = line * scale
            if k:
                line = pltpu.roll(line, LANES - BLOCK * k, axis=1)
            flat[pl.ds(((z // 8) * BLOCK + k * 8) * 8 + z % 8, 8, stride=8), :] = line


def volume(plan, phases, begin, count, previous=None):
    na, nz, span = phases.shape
    base, index, frac = plan
    n = NG // BLOCK
    rows = n * na * 8
    steps = lambda i: (i + begin, 0)
    specs = [
        pl.BlockSpec(memory_space=pltpu.SMEM),
        pl.BlockSpec((na, nz, span), lambda i: (0, 0, 0)),
        pl.BlockSpec((rows, LANES), steps),
        pl.BlockSpec((rows, LANES), steps),
    ]
    args = [base, phases, index, frac]
    alias = {}
    if previous is not None:
        specs.append(pl.BlockSpec(memory_space=pl.ANY))
        args.append(previous)
        alias = {4: 0}
    return pl.pallas_call(
        functools.partial(volume_kernel, begin=begin),
        grid=(count,),
        in_specs=specs,
        out_specs=pl.BlockSpec((nz // 8, BLOCK, 8, LANES), lambda i: (0, i + begin, 0, 0)),
        out_shape=jax.ShapeDtypeStruct((nz // 8, NG, 8, LANES), F32),
        input_output_aliases=alias,
        scratch_shapes=[
            pltpu.VMEM((na * n, nz, span), jnp.int32),
            pltpu.VMEM((nz, LANES), F32),
            pltpu.VMEM((n, nz, 8, LANES), F32),
        ],
        compiler_params=pltpu.CompilerParams(vmem_limit_bytes=VMEM_LIMIT),
        cost_estimate=pl.CostEstimate(flops=count << 25, bytes_accessed=count << 21, transcendentals=0),
    )(*args)


def swap(value, axis, stride):
    count = lax.axis_size(axis)
    return lax.ppermute(value, axis, [(i, i ^ stride) for i in range(count)])


def halves(value, axis, stride):
    bit = (lax.axis_index(axis) // stride) % 2
    pick = lambda at: lax.dynamic_index_in_dim(value, at, 0, keepdims=False)
    return pick(bit), pick(1 - bit), bit


def exchange_angles(value):
    stride = lax.axis_size("angle") // 2
    slots = [value]
    while stride:
        kept, sent = [], []
        for v in slots:
            mine, other, _ = halves(v.reshape((2, v.shape[0] // 2) + v.shape[1:]), "angle", stride)
            kept.append(mine)
            sent.append(other)
        got = swap(jnp.stack(sent), "angle", stride)
        slots = kept + [got[i] for i in range(len(sent))]
        stride //= 2
    bits = len(slots).bit_length() - 1
    order = [int(format(j, f"0{bits}b")[::-1], 2) for j in range(len(slots))]
    return jnp.stack([slots[j][0] for j in order])


def sum_everywhere(kept, sent):
    mine, other = fold(kept, swap(sent, "strip", 1))
    value = mine + swap(other, "angle", 1).astype(F32)
    stages = [("angle", 1 << k) for k in range(1, lax.axis_size("angle").bit_length() - 1)]
    stages += [("strip", 1 << k) for k in range(1, lax.axis_size("strip").bit_length() - 1)]
    for axis, stride in stages:
        rounded = value.astype(BF16)
        value = rounded.astype(F32) + swap(rounded, axis, stride).astype(F32)
    value = value.astype(BF16)
    for axis, stride in (("angle", 1), ("strip", 1)):
        got = swap(value, axis, stride)
        bit = lax.axis_index(axis) % 2
        value = jnp.where(bit == 0, jnp.stack([value, got]), jnp.stack([got, value]))
        if axis == "angle":
            value = value.reshape((-1,) + value.shape[2:])
    return value.astype(F32)


def shards(object_field, amplitudes, scan_offsets, probe_field, tilt_angles):
    strip_rows = object_field.shape[2]
    width = object_field.shape[3]
    angles = lax.axis_size("angle")
    strips = lax.axis_size("strip")
    assert strips % 2 == 0 and strips & (strips - 1) == 0 and angles & (angles - 1) == 0 and angles > 1
    reach = math.sqrt(2.0) * (NG - 1)
    lo = int(math.floor((width - 1) / 2.0 - reach - 1)) // HALO * HALO
    span = -(-int(math.ceil((width - 1) / 2.0 + reach + 2) - lo) // LANES) * LANES
    assert 0 <= lo and lo + span <= width and NG == LANES
    wlo = lo // LANES * LANES
    whi = -(-(lo + span) // LANES) * LANES

    beside = [(i, i + 1 if i % 2 else i - 1) for i in range(1, strips - 1)]

    def far_swap(value):
        return lax.ppermute(value, "strip", beside)

    own = object_field[:, 0]
    odd = lax.axis_index("strip") % 2
    half = lambda at: lax.dynamic_slice_in_dim(own, at * HALO, HALO, 1).astype(BF16)
    far, own = lax.optimization_barrier((half(odd), own))
    near, *inputs = lax.optimization_barrier((half(1 - odd), own, probe_field, amplitudes[0]))
    far = far_swap(far)
    near = swap(near, "strip", 1)

    me = lax.axis_index("angle")
    theta = jnp.take(tilt_angles, me ^ jnp.arange(angles, dtype=jnp.int32))
    plan = detector_plan(theta, width, lo, span)

    tables = jnp.asarray(dft_tables(amplitudes.shape[2]))
    inputs, plan, columns = lax.optimization_barrier((inputs, plan, scan_offsets[0, :, 1]))
    inputs = fetch(*inputs, tables)
    view = inputs[0]
    core, rnear, rfar, kept, sent = frames(columns, near, far, *inputs, wlo, whi)
    rfar = far_swap(rfar)
    rnear = swap(rnear, "strip", 1)
    phase = merged_phase(view, core, rnear, rfar, lo, span, wlo, whi)
    object_grad = merged_grad(core, rnear, rfar)
    phases = exchange_angles(phase.reshape(angles, strip_rows // angles, span))
    blocks = NG // BLOCK
    result = None
    for part in range(PARTS):
        result = volume(plan, phases, part * blocks // PARTS, blocks // PARTS, result)
    slices = strip_rows // angles
    result = result.transpose(0, 2, 1, 3).reshape(1, 1, slices, NG * NG)

    frames_all = angles * strips * scan_offsets.shape[1]
    probe_grad = sum_everywhere(kept, sent) * (1.0 / math.sqrt(frames_all))
    return object_grad[:, None], probe_grad, result


def solution(mesh):
    return jax.shard_map(
        shards,
        mesh=mesh,
        in_specs=(
            P(None, "angle", "strip", None),
            P("angle", "strip", None, None),
            P("angle", "strip", None),
            P(),
            P(),
        ),
        out_specs=(P(None, "angle", "strip", None), P(), P("strip", "angle", None, None)),
        check_vma=False,
    )
```

```python
import functools
import math

import jax
import jax.numpy as jnp
import numpy as np
from jax import lax
from jax.experimental import pallas as pl
from jax.experimental.pallas import tpu as pltpu
from jax.sharding import PartitionSpec as P

HALO = 64
NG = 128
LANES = 128
BLOCK = 32
PARTS = 2
VMEM_LIMIT = 20 << 20
FETCH_LIMIT = 20 << 20
F32 = jnp.float32
BF16 = jnp.bfloat16


def dft_tables(size):
    k = np.arange(size)
    arg = 2.0 * np.pi / size * ((k[:, None] * k[None, :]) % size)
    tables = np.stack([np.cos(arg), np.sin(arg)]) / math.sqrt(size)
    return tables.astype(np.float32).astype(jnp.bfloat16)


def frames_kernel(col_ref, near_ref, far_ref, own_ref, probe_ref, amp_ref, tab_ref,
                  core_ref, rnear_ref, rfar_ref, kept_ref, sent_ref, ext_ref, grad_ref, pterm_ref, fwd_ref, inv_ref, *, wlo, whi):
    nf, n, _ = amp_ref.shape
    rows = own_ref.shape[1]
    width = own_ref.shape[2]
    wide = n + LANES
    odd = lax.axis_index("strip") % 2
    below = HALO + rows
    near_row = pl.multiple_of(jnp.where(odd == 0, below, 0), HALO)
    far_row = pl.multiple_of(jnp.where(odd == 0, 0, below), HALO)
    ext_ref[:, HALO:below] = own_ref[...]
    cos, sin = tab_ref[0], tab_ref[1]
    fwd_ref[:n, :n] = cos
    fwd_ref[:n, n:] = sin
    fwd_ref[n:, :n] = -sin
    fwd_ref[n:, n:] = cos
    inv_ref[:n, :n] = cos
    inv_ref[:n, n:] = -sin
    inv_ref[n:, :n] = sin
    inv_ref[n:, n:] = cos
    grad_ref[...] = jnp.zeros_like(grad_ref)
    pterm_ref[...] = jnp.zeros_like(pterm_ref)
    ext_ref[:, pl.ds(near_row, HALO)] = near_ref[...].astype(F32)
    ext_ref[:, pl.ds(far_row, HALO)] = far_ref[...].astype(F32)
    static_cols = (width - n, 0, (width - n) // 2)
    for f in range(nf):
        if f < 3 and static_cols[f] % LANES == 0:
            col, shift = static_cols[f], None
            patch_re = ext_ref[0, :, col : col + n]
            patch_im = ext_ref[1, :, col : col + n]
        else:
            at = col_ref[f]
            base = pl.multiple_of(jnp.minimum((at >> 7) * LANES, width - wide), LANES)
            shift = at - base
            patch_re = pltpu.roll(ext_ref[0, :, pl.ds(base, wide)], wide - shift, axis=1)[:, :n]
            patch_im = pltpu.roll(ext_ref[1, :, pl.ds(base, wide)], wide - shift, axis=1)[:, :n]
        probe_re, probe_im = probe_ref[0], probe_ref[1]
        exit_wave = jnp.concatenate(
            [probe_re * patch_re - probe_im * patch_im, probe_re * patch_im + probe_im * patch_re], 0
        ).astype(BF16)
        half = jnp.dot(fwd_ref[...], exit_wave, preferred_element_type=F32).astype(BF16)
        half = jnp.concatenate([half[:n], half[n:]], 1)
        wave = jnp.dot(half, inv_ref[...], preferred_element_type=F32)
        wave_re, wave_im = wave[:, :n], wave[:, n:]
        factor = 1.0 - amp_ref[f].astype(F32) * lax.rsqrt(wave_re * wave_re + wave_im * wave_im + 1.0)
        misfit = jnp.concatenate([wave_re * factor, wave_im * factor], 0).astype(BF16)
        back = jnp.dot(inv_ref[...], misfit, preferred_element_type=F32).astype(BF16)
        back = jnp.concatenate([back[:n], back[n:]], 1)
        grad = jnp.dot(back, fwd_ref[...], preferred_element_type=F32)
        grad_re, grad_im = grad[:, :n], grad[:, n:]
        pterm_ref[0] += patch_re * grad_re + patch_im * grad_im
        pterm_ref[1] += patch_re * grad_im - patch_im * grad_re
        terms = (probe_re * grad_re + probe_im * grad_im, probe_re * grad_im - probe_im * grad_re)
        for k in range(2):
            if shift is None:
                grad_ref[k, :, col : col + n] += terms[k]
            else:
                padded = jnp.concatenate([terms[k], jnp.zeros((n, LANES), F32)], 1)
                grad_ref[k, :, pl.ds(base, wide)] += pltpu.roll(padded, shift, axis=1)

    sent_ref[...] = pterm_ref[1 - odd].astype(BF16)
    kept_ref[...] = pterm_ref[odd]
    rnear_ref[...] = grad_ref[:, pl.ds(near_row, HALO)].astype(BF16)
    rfar_ref[...] = grad_ref[:, pl.ds(far_row, HALO)].astype(BF16)
    core_ref[...] = grad_ref[:, HALO:below]


def in_vmem(count):
    return [pl.BlockSpec(memory_space=pltpu.VMEM)] * count


def fetch_kernel(*refs):
    sems = refs[-1]
    count = (len(refs) - 1) // 2
    copies = [pltpu.make_async_copy(refs[k], refs[count + k], sems.at[k]) for k in range(count)]
    for copy in copies:
        copy.start()
    for copy in copies:
        copy.wait()


def fetch(*arrays):
    size = sum(x.size * x.dtype.itemsize for x in arrays)
    return pl.pallas_call(
        fetch_kernel,
        in_specs=[pl.BlockSpec(memory_space=pltpu.HBM)] * len(arrays),
        out_specs=in_vmem(len(arrays)),
        out_shape=[jax.ShapeDtypeStruct(x.shape, x.dtype) for x in arrays],
        scratch_shapes=[pltpu.SemaphoreType.DMA((len(arrays),))],
        compiler_params=pltpu.CompilerParams(vmem_limit_bytes=FETCH_LIMIT),
        cost_estimate=pl.CostEstimate(flops=0, bytes_accessed=size, transcendentals=0),
        name="fetch",
    )(*arrays)


def frames(columns, near, far, own, probe, amps, tables, wlo, whi):
    nf, n, _ = amps.shape
    _, rows, width = own.shape
    ext = rows + 2 * HALO
    assert ext == n and rows == 2 * HALO
    args = (near, far, own, probe, amps, tables)
    outs = [
        jax.ShapeDtypeStruct(own.shape, F32),
        jax.ShapeDtypeStruct((2, HALO, width), BF16),
        jax.ShapeDtypeStruct((2, HALO, width), BF16),
        jax.ShapeDtypeStruct((n, n), F32),
        jax.ShapeDtypeStruct((n, n), BF16),
    ]
    return pl.pallas_call(
        functools.partial(frames_kernel, wlo=wlo, whi=whi),
        in_specs=[pl.BlockSpec(memory_space=pltpu.SMEM)] + in_vmem(6),
        out_specs=in_vmem(len(outs)),
        out_shape=outs,
        scratch_shapes=[
            pltpu.VMEM((2, ext, width), F32),
            pltpu.VMEM((2, ext, width), F32),
            pltpu.VMEM((2, n, n), F32),
            pltpu.VMEM((2 * n, 2 * n), BF16),
            pltpu.VMEM((2 * n, 2 * n), BF16),
        ],
        compiler_params=pltpu.CompilerParams(vmem_limit_bytes=VMEM_LIMIT),
        cost_estimate=pl.CostEstimate(flops=64 * nf * n**3, bytes_accessed=6 << 20, transcendentals=nf * n * n),
        name="frames",
    )(columns, *args)


def phase_kernel(view_ref, core_ref, near_ref, far_ref, phase_ref, *, lo, wlo, whi):
    rows = view_ref.shape[1]
    span = phase_ref.shape[1]
    odd = lax.axis_index("strip") % 2
    for rim_ref, parity in ((near_ref, odd), (far_ref, 1 - odd)):
        at = pl.ds(pl.multiple_of(jnp.where(parity == 0, rows - HALO, 0), HALO), HALO)
        grad_re = core_ref[0, at, wlo:whi] + rim_ref[0, :, wlo:whi].astype(F32)
        grad_im = core_ref[1, at, wlo:whi] + rim_ref[1, :, wlo:whi].astype(F32)
        phase = view_ref[0, at, wlo:whi] * grad_im - view_ref[1, at, wlo:whi] * grad_re
        if lo > wlo:
            phase = pltpu.roll(phase, whi - lo, axis=1)
        phase_ref[at] = phase[:, :span].astype(BF16)


def merged_phase(view, core, near, far, lo, span, wlo, whi):
    return pl.pallas_call(
        functools.partial(phase_kernel, lo=lo, wlo=wlo, whi=whi),
        in_specs=in_vmem(4),
        out_specs=pl.BlockSpec(memory_space=pltpu.VMEM),
        out_shape=jax.ShapeDtypeStruct((view.shape[1], span), BF16),
        compiler_params=pltpu.CompilerParams(vmem_limit_bytes=VMEM_LIMIT),
        cost_estimate=pl.CostEstimate(flops=1 << 19, bytes_accessed=1 << 20, transcendentals=0),
        name="phase",
    )(view, core, near, far)


def rim_kernel(core_ref, near_ref, far_ref, grad_ref):
    rows = core_ref.shape[1]
    odd = lax.axis_index("strip") % 2
    for rim_ref, parity in ((near_ref, odd), (far_ref, 1 - odd)):
        at = pl.ds(pl.multiple_of(jnp.where(parity == 0, rows - HALO, 0), HALO), HALO)
        grad_ref[:, at] = core_ref[:, at] + rim_ref[...].astype(F32)


def merged_grad(core, near, far):
    return pl.pallas_call(
        rim_kernel,
        in_specs=in_vmem(3),
        out_specs=pl.BlockSpec(memory_space=pltpu.VMEM),
        out_shape=jax.ShapeDtypeStruct(core.shape, F32),
        compiler_params=pltpu.CompilerParams(vmem_limit_bytes=VMEM_LIMIT),
        cost_estimate=pl.CostEstimate(flops=1 << 18, bytes_accessed=2 << 20, transcendentals=0),
        name="rims",
    )(core, near, far)


def fold_kernel(kept_ref, got_ref, mine_ref, other_ref):
    rows = mine_ref.shape[0]
    bit = lax.axis_index("angle") % 2
    for out_ref, which in ((other_ref, 1 - bit), (mine_ref, bit)):
        at = pl.ds(pl.multiple_of(which * rows, rows), rows)
        out_ref[...] = (kept_ref[at] + got_ref[at].astype(F32)).astype(out_ref.dtype)


def fold(kept, got):
    shape = (kept.shape[0] // 2, kept.shape[1])
    return pl.pallas_call(
        fold_kernel,
        in_specs=in_vmem(2),
        out_specs=in_vmem(2),
        out_shape=[jax.ShapeDtypeStruct(shape, F32), jax.ShapeDtypeStruct(shape, BF16)],
        compiler_params=pltpu.CompilerParams(vmem_limit_bytes=VMEM_LIMIT),
        cost_estimate=pl.CostEstimate(flops=kept.size, bytes_accessed=8 * kept.size, transcendentals=0),
        name="fold",
    )(kept, got)


def detector_plan(theta, width, lo, span):
    center = (NG - 1) / 2.0
    n = NG // BLOCK
    c = jnp.cos(theta)[None, None, :]
    s = jnp.sin(theta)[None, None, :]
    x0 = (jnp.arange(n, dtype=F32) * BLOCK - center)[:, None, None]
    y0 = (jnp.arange(n, dtype=F32) * BLOCK - center)[None, :, None]
    first = (width - 1) / 2.0 - lo + 2.0 * (
        x0 * c + jnp.minimum(0.0, (BLOCK - 1) * c) + y0 * s + jnp.minimum(0.0, (BLOCK - 1) * s)
    )
    base = jnp.clip(jnp.floor((first - 1.0 / 64) / BLOCK), 0, span // BLOCK - 1) * BLOCK
    sub = jnp.arange(8, dtype=jnp.int32)[:, None]
    lane = jnp.arange(LANES, dtype=jnp.int32)[None, :]
    yblock = jnp.arange(n, dtype=jnp.int32)[:, None, None]
    xin = ((lane // BLOCK - yblock) % n * 8 + sub[None]).astype(F32)
    yin = (lane % BLOCK).astype(F32)[None]
    xpos = x0[:, :, :, None, None] + xin[None, :, None]
    ypos = y0[:, :, :, None, None] + yin[None, :, None]
    upos = (width - 1) / 2.0 + 2.0 * (xpos * c[..., None, None] + ypos * s[..., None, None])
    lower = jnp.clip(jnp.floor(upos), 0.0, width - 2.0)
    frac = upos - lower
    local = (lower - lo - base[..., None, None]).astype(jnp.int32) & (LANES - 1)
    flat = n * n * theta.shape[0] * 8
    return base.astype(jnp.int32).reshape(-1), local.reshape(flat, LANES), frac.reshape(flat, LANES)


GATHER_LANES = lax.GatherDimensionNumbers(
    offset_dims=(),
    collapsed_slice_dims=(1,),
    start_index_map=(1,),
    operand_batching_dims=(0,),
    start_indices_batching_dims=(0,),
)


def lane_gather(table, index):
    return lax.gather(
        table, index[..., None], GATHER_LANES, slice_sizes=(1, 1),
        mode=lax.GatherScatterMode.PROMISE_IN_BOUNDS,
    )


def volume_kernel(base_ref, phase_ref, index_ref, frac_ref, *refs, begin):
    out_ref, tab_ref, scale_ref, part_ref = refs[-4:]
    na, nz, span = phase_ref.shape
    n = NG // BLOCK
    top = float(32767 // na)
    zc = min(16, nz)
    step = pl.program_id(0)

    @pl.when(step == 0)
    def _():
        values = [phase_ref[a].astype(F32) for a in range(na)]
        peak = functools.reduce(
            jnp.maximum, [jnp.max(jnp.abs(v), axis=1, keepdims=True) for v in values]
        )
        scale = jnp.where(peak > 0, top / peak, 0.0)
        scale_ref[...] = jnp.broadcast_to(peak * (1.0 / (top * 65536.0)), (nz, LANES))
        for a in range(na):
            q = jnp.round(values[a] * scale).astype(jnp.int32)
            packed = ((pltpu.roll(q, span - 1, axis=1) - q) << 16) + q
            for k in range(n):
                tab_ref[a * n + k] = packed if k == 0 else pltpu.roll(packed, span - BLOCK * k, axis=1)

    for z0 in range(0, nz, zc):
        for yb in range(n):
            sums = [None] * zc
            for a in range(na):
                base = base_ref[((begin + step) * n + yb) * na + a]
                copy = a * n + (base // BLOCK) % n
                tile = pl.multiple_of(base // LANES * LANES, LANES)
                row = (yb * na + a) * 8
                index = index_ref[row : row + 8, :]
                frac = frac_ref[row : row + 8, :]
                for i in range(zc):
                    line = tab_ref[copy, z0 + i : z0 + i + 1, pl.ds(tile, LANES)]
                    packed = lane_gather(jnp.broadcast_to(line, (8, LANES)), index)
                    slope = frac * packed.astype(F32)
                    sums[i] = (packed, slope) if a == 0 else (sums[i][0] + packed, sums[i][1] + slope)
            for i in range(zc):
                part_ref[yb, z0 + i] = (sums[i][0] << 16).astype(F32) + sums[i][1]
    flat = out_ref.reshape(nz * BLOCK, LANES)
    block = lax.broadcasted_iota(jnp.int32, (8, LANES), 1) // BLOCK
    for z in range(nz):
        parts = [part_ref[yb, z] for yb in range(n)]
        scale = jnp.broadcast_to(scale_ref[z : z + 1, :], (8, LANES))
        for k in range(n):
            line = parts[-k % n]
            for p in range(1, n):
                line = jnp.where(block == p, parts[(p - k) % n], line)
            line = line * scale
            if k:
                line = pltpu.roll(line, LANES - BLOCK * k, axis=1)
            flat[pl.ds(((z // 8) * BLOCK + k * 8) * 8 + z % 8, 8, stride=8), :] = line


def volume(plan, phases, begin, count, previous=None):
    na, nz, span = phases.shape
    base, index, frac = plan
    n = NG // BLOCK
    rows = n * na * 8
    steps = lambda i: (i + begin, 0)
    specs = [
        pl.BlockSpec(memory_space=pltpu.SMEM),
        pl.BlockSpec((na, nz, span), lambda i: (0, 0, 0)),
        pl.BlockSpec((rows, LANES), steps),
        pl.BlockSpec((rows, LANES), steps),
    ]
    args = [base, phases, index, frac]
    alias = {}
    if previous is not None:
        specs.append(pl.BlockSpec(memory_space=pl.ANY))
        args.append(previous)
        alias = {4: 0}
    return pl.pallas_call(
        functools.partial(volume_kernel, begin=begin),
        grid=(count,),
        in_specs=specs,
        out_specs=pl.BlockSpec((nz // 8, BLOCK, 8, LANES), lambda i: (0, i + begin, 0, 0)),
        out_shape=jax.ShapeDtypeStruct((nz // 8, NG, 8, LANES), F32),
        input_output_aliases=alias,
        scratch_shapes=[
            pltpu.VMEM((na * n, nz, span), jnp.int32),
            pltpu.VMEM((nz, LANES), F32),
            pltpu.VMEM((n, nz, 8, LANES), F32),
        ],
        compiler_params=pltpu.CompilerParams(vmem_limit_bytes=VMEM_LIMIT),
        cost_estimate=pl.CostEstimate(flops=count << 25, bytes_accessed=count << 21, transcendentals=0),
    )(*args)


def swap(value, axis, stride):
    count = lax.axis_size(axis)
    return lax.ppermute(value, axis, [(i, i ^ stride) for i in range(count)])


def exchange_angles(value):
    slots = [value]
    for k in range(lax.axis_size("angle").bit_length() - 1):
        bit = (lax.axis_index("angle") >> k) % 2
        kept, sent = [], []
        for v in slots:
            v = v.reshape((v.shape[0] // 2, 2) + v.shape[1:])
            kept.append(lax.dynamic_index_in_dim(v, bit, 1, keepdims=False))
            sent.append(lax.dynamic_index_in_dim(v, 1 - bit, 1, keepdims=False))
        got = swap(jnp.stack(sent), "angle", 1 << k)
        slots = kept + [got[i] for i in range(len(sent))]
    return jnp.stack([v[0] for v in slots])


def sum_everywhere(kept, sent):
    mine, other = fold(kept, swap(sent, "strip", 1))
    value = mine + swap(other, "angle", 1).astype(F32)
    stages = [("angle", 1 << k) for k in range(1, lax.axis_size("angle").bit_length() - 1)]
    stages += [("strip", 1 << k) for k in range(1, lax.axis_size("strip").bit_length() - 1)]
    for axis, stride in stages:
        rounded = value.astype(BF16)
        value = rounded.astype(F32) + swap(rounded, axis, stride).astype(F32)
    value = value.astype(BF16)
    for axis, stride in (("angle", 1), ("strip", 1)):
        got = swap(value, axis, stride)
        bit = lax.axis_index(axis) % 2
        value = jnp.where(bit == 0, jnp.stack([value, got]), jnp.stack([got, value]))
        if axis == "angle":
            value = value.reshape((-1,) + value.shape[2:])
    return value.astype(F32)


def shards(object_field, amplitudes, scan_offsets, probe_field, tilt_angles):
    strip_rows = object_field.shape[2]
    width = object_field.shape[3]
    angles = lax.axis_size("angle")
    strips = lax.axis_size("strip")
    assert strips % 2 == 0 and strips & (strips - 1) == 0 and angles & (angles - 1) == 0 and angles > 1
    reach = math.sqrt(2.0) * (NG - 1)
    lo = int(math.floor((width - 1) / 2.0 - reach - 1)) // HALO * HALO
    span = -(-int(math.ceil((width - 1) / 2.0 + reach + 2) - lo) // LANES) * LANES
    assert 0 <= lo and lo + span <= width and NG == LANES
    wlo = lo // LANES * LANES
    whi = -(-(lo + span) // LANES) * LANES

    beside = [(i, i + 1 if i % 2 else i - 1) for i in range(1, strips - 1)]

    def far_swap(value):
        return lax.ppermute(value, "strip", beside)

    own = object_field[:, 0]
    odd = lax.axis_index("strip") % 2
    half = lambda at: lax.dynamic_slice_in_dim(own, at * HALO, HALO, 1).astype(BF16)
    far, own = lax.optimization_barrier((half(odd), own))
    near, *inputs = lax.optimization_barrier((half(1 - odd), own, probe_field, amplitudes[0]))
    far = far_swap(far)
    near = swap(near, "strip", 1)

    me = lax.axis_index("angle")
    theta = jnp.take(tilt_angles, me ^ jnp.arange(angles, dtype=jnp.int32))
    plan = detector_plan(theta, width, lo, span)

    tables = jnp.asarray(dft_tables(amplitudes.shape[2]))
    inputs, plan, columns = lax.optimization_barrier((inputs, plan, scan_offsets[0, :, 1]))
    inputs = fetch(*inputs, tables)
    view = inputs[0]
    core, rnear, rfar, kept, sent = frames(columns, near, far, *inputs, wlo, whi)
    rfar = far_swap(rfar)
    rnear = swap(rnear, "strip", 1)
    phase = merged_phase(view, core, rnear, rfar, lo, span, wlo, whi)
    object_grad = merged_grad(core, rnear, rfar)
    phases = exchange_angles(phase.reshape(angles, strip_rows // angles, span))
    blocks = NG // BLOCK
    result = None
    for part in range(PARTS):
        result = volume(plan, phases, part * blocks // PARTS, blocks // PARTS, result)
    slices = strip_rows // angles
    result = result.transpose(0, 2, 1, 3).reshape(1, 1, slices, NG * NG)

    frames_all = angles * strips * scan_offsets.shape[1]
    probe_grad = sum_everywhere(kept, sent) * (1.0 / math.sqrt(frames_all))
    return object_grad[:, None], probe_grad, result


def solution(mesh):
    return jax.shard_map(
        shards,
        mesh=mesh,
        in_specs=(
            P(None, "angle", "strip", None),
            P("angle", "strip", None, None),
            P("angle", "strip", None),
            P(),
            P(),
        ),
        out_specs=(P(None, "angle", "strip", None), P(), P("strip", "angle", None, None)),
        check_vma=False,
    )
```
